128 devices in a mesh: row: 16 (over z, x_lo, core), col: 8 (over y, x_hi).
Axes of the slice: x: 4 (x_hi: 2, x_lo: 2; x = x_hi * 2 + x_lo), y: 4, z: 4, core: 2. Of those that a mesh axis runs over, the one named last changes fastest.
Arguments:
- layer_input: bfloat16 [4096, 8192], P('row', 'col'), may hold values from -6 to 6
- attn_grad: bfloat16 [4096, 8192], P('row', 'col'), may hold values from -6 to 6
- queries: bfloat16 [16, 256, 8192], P('row', None, 'col'), may hold values from -6 to 6
- keys: bfloat16 [16, 256, 8192], P('row', None, 'col'), may hold values from -6 to 6
- values: bfloat16 [16, 256, 8192], P('row', None, 'col'), may hold values from -6 to 6
- masked: int32 [16, 256], P('row'), may hold values 0 or 1
- key_bias: float32 [64], P('col'), may hold values from -2 to 2
- w_query: bfloat16 [8192, 8192], P('row', 'col'), may hold values from -0.0625 to 0.0625
- w_key: bfloat16 [8192, 8192], P('row', 'col'), may hold values from -0.0625 to 0.0625
- w_value: bfloat16 [8192, 8192], P('row', 'col'), may hold values from -0.0625 to 0.0625
Outputs:
- layer_grad: bfloat16 [4096, 8192], P('row', 'col')
- w_query_grad: bfloat16 [8192, 8192], P('row', 'col')
- w_key_grad: bfloat16 [8192, 8192], P('row', 'col')
- w_value_grad: bfloat16 [8192, 8192], P('row', 'col')
- bias_grad: float32 [64], P('col')
The draws below stay inside these ranges and needn't reach their ends.
All inputs are finite; a program needn't handle non-finite values. No bound on the sum of `masked` on one device may be relied on, other than what follows from the above.
Results may differ from the reference program's by a relative error of at most 0.015.
Values may be sent and summed in bfloat16 or wider, within the bound.
A program may use at most 192 MiB of HBM per device.

```python
import jax
import jax.numpy as jnp
from jax import lax

D = 8192
HEADS = 64
SEQ = 256
HD = 128
CANV = 16
TOKENS = 4096
N_COL = 8


def shared_draw(key):
    folded = jax.random.fold_in(key, 7101)
    key_query, key_keys = jax.random.split(folded, 2)
    head_dim = D // HEADS
    grid_shape = (CANV, SEQ, HEADS, head_dim)
    query_vals = jnp.clip(jax.random.normal(key_query, grid_shape, jnp.float32), -4.5, 4.5)
    key_vals = jnp.clip(jax.random.normal(key_keys, grid_shape, jnp.float32), -4.5, 4.5)
    return (query_vals.reshape(CANV, SEQ, D), key_vals.reshape(CANV, SEQ, D))


def draw_queries(key, part):
    return shared_draw(key)[0].astype(jnp.bfloat16)


def draw_keys(key, part):
    return shared_draw(key)[1].astype(jnp.bfloat16)


def place_ends(array, rng, least, high):
    place = [jax.random.randint(jax.random.fold_in(rng, axis), (), 0, length) for axis, length in enumerate(array.shape)]
    widest = array.shape.index(max(array.shape))
    next_to = place[:widest] + [(place[widest] + 1) % array.shape[widest]] + place[widest + 1:]
    return array.at[tuple(place)].set(least).at[tuple(next_to)].set(high)


def shard_levels(rng, extent, shards, least, high):
    gain = 1.0
    for position, shards_of in shards:
        draws = jax.random.uniform(jax.random.fold_in(jax.random.fold_in(rng, 6), position), (shards_of,), jnp.float32, least / len(shards), high / len(shards))
        gain = gain * jnp.repeat(jnp.exp(draws), extent[position] // shards_of).reshape((-1,) + (1,) * (len(extent) - 1 - position))
    return gain


def normal_values(own_key, extent, spread, limit, cuts=(), dtype=jnp.bfloat16):
    gain = shard_levels(own_key, extent, cuts, -0.22, 0.18) if cuts else 1.0
    entries = jax.random.normal(own_key, extent, jnp.float32) * spread * gain
    return jnp.minimum(jnp.maximum(entries, -limit), limit).astype(dtype)


def setup_inputs(seed: int = 0) -> dict:
    streams_of = jax.random.split(jax.random.key(seed), 11)
    return {
        "layer_input": normal_values(streams_of[0], (TOKENS, D), 1.0, 6.0, ((0, 16), (1, 8))),
        "attn_grad": normal_values(streams_of[1], (TOKENS, D), 1.0, 6.0, ((0, 16), (1, 8))),
        "queries": draw_queries(jax.random.fold_in(streams_of[10], 71), 0),
        "keys": draw_keys(jax.random.fold_in(streams_of[10], 71), 0),
        "values": normal_values(streams_of[4], (CANV, SEQ, D), 1.0, 6.0, ((0, 16), (2, 8))),
        "masked": place_ends((jax.random.randint(streams_of[5], (CANV, SEQ), 0, 2) < 1).astype(jnp.int32), jax.random.fold_in(streams_of[5], 1), 0, 1),
        "key_bias": jnp.clip(jax.random.uniform(streams_of[6], (HEADS,), jnp.float32, -2.0, 2.0) * shard_levels(streams_of[6], (HEADS,), ((0, 8),), -0.4, 0.0), -2.0, 2.0),
        "w_query": normal_values(streams_of[7], (D, D), D ** -0.5, 0.0625, ((0, 16), (1, 8))),
        "w_key": normal_values(streams_of[8], (D, D), D ** -0.5, 0.0625, ((0, 16), (1, 8))),
        "w_value": normal_values(streams_of[9], (D, D), D ** -0.5, 0.0625, ((0, 16), (1, 8))),
    }


def canvas_backward(query_c, key_c, value_c, grad_c, flag_c, key_bias):
    scale_qk = 1.0 / jnp.sqrt(jnp.float32(HD))
    query_h = query_c.reshape(SEQ, HEADS, HD).astype(jnp.float32)
    key_h = key_c.reshape(SEQ, HEADS, HD).astype(jnp.float32)
    value_h = value_c.reshape(SEQ, HEADS, HD).astype(jnp.float32)
    grad_h = grad_c.reshape(SEQ, HEADS, HD).astype(jnp.float32)
    flag_float = flag_c.astype(jnp.float32)
    scores = jnp.einsum('ihd,jhd->hij', query_h, key_h) * scale_qk + key_bias[:, None, None] * flag_float[None, None, :]
    row_max = lax.optimization_barrier(jnp.max(scores, axis=-1, keepdims=True))
    exp_terms = jnp.exp(scores - row_max)
    attn_probs = exp_terms / lax.optimization_barrier(jnp.sum(exp_terms, axis=-1, keepdims=True))
    probs_low = lax.optimization_barrier(attn_probs.astype(jnp.bfloat16)).astype(jnp.float32)
    attended = jnp.einsum('hij,jhd->ihd', probs_low, value_h)
    delta = lax.optimization_barrier(jnp.sum(grad_h * attended, axis=-1))
    grad_probs = jnp.einsum('ihd,jhd->hij', grad_h, value_h)
    grad_scores = attn_probs * (grad_probs - jnp.transpose(delta)[:, :, None])
    grad_low = lax.optimization_barrier(grad_scores.astype(jnp.bfloat16)).astype(jnp.float32)
    value_grad = jnp.einsum('hij,ihd->jhd', probs_low, grad_h).astype(jnp.bfloat16)
    query_grad = (jnp.einsum('hij,jhd->ihd', grad_low, key_h) * scale_qk).astype(jnp.bfloat16)
    key_grad = (jnp.einsum('hij,ihd->jhd', grad_low, query_h) * scale_qk).astype(jnp.bfloat16)
    bias_part = lax.optimization_barrier(jnp.sum(grad_scores * flag_float[None, None, :], axis=(1, 2)))
    return (query_grad.reshape(SEQ, D), key_grad.reshape(SEQ, D), value_grad.reshape(SEQ, D), bias_part)

def reference(layer_input, attn_grad, queries, keys, values, masked, key_bias, w_query, w_key, w_value):
    grad_canvas = attn_grad.reshape(CANV, SEQ, D)

    def one_canvas(inputs_one):
        return canvas_backward(inputs_one[0], inputs_one[1], inputs_one[2], inputs_one[3], inputs_one[4], key_bias)
    query_grad, key_grad, value_grad, bias_parts = lax.map(one_canvas, (queries, keys, values, grad_canvas, masked))
    bias_grad = lax.optimization_barrier(jnp.sum(bias_parts, axis=0))
    flat_grads = (query_grad.reshape(TOKENS, D), key_grad.reshape(TOKENS, D), value_grad.reshape(TOKENS, D))
    weights = (w_query, w_key, w_value)
    input_t = layer_input.T
    weight_grads = [jnp.dot(input_t, member, preferred_element_type=jnp.float32).astype(jnp.bfloat16) for member in flat_grads]
    width_col = D // N_COL
    accumulated = jnp.zeros((TOKENS, D), jnp.float32)
    for column in range(N_COL):
        col_start = column * width_col
        col_part = jnp.zeros((TOKENS, D), jnp.float32)
        for member, weight in zip(flat_grads, weights):
            col_part = col_part + jnp.dot(member[:, col_start:col_start + width_col], weight[:, col_start:col_start + width_col].T, preferred_element_type=jnp.float32)
        accumulated = accumulated + lax.optimization_barrier(col_part.astype(jnp.bfloat16)).astype(jnp.float32)
    layer_grad = accumulated.astype(jnp.bfloat16)
    return (layer_grad, weight_grads[0], weight_grads[1], weight_grads[2], bias_grad)
```

```python
import functools

import jax
import jax.numpy as jnp
from jax import lax
from jax.experimental import pallas as pl
from jax.experimental.pallas import tpu as pltpu
from jax.sharding import PartitionSpec as P

BF = jnp.bfloat16
F32 = jnp.float32
MESH_ID = pl.DeviceIdType.MESH

ROWS, COLS = 16, 8
TOK, WIDTH, DEPTH = 256, 1024, 512
HEADS, HD = 8, 128
HALF = TOK // 2
PAIRS = 8
NT = (((1,), (1,)), ((), ()))
TN = (((0,), (0,)), ((), ()))
NN = (((1,), (0,)), ((), ()))

Z_FIRST = (0, 1)
ALL = (0, 1, 2, 3, 4, 5)
X_FIRST = tuple(ch for ch in ALL if ch not in Z_FIRST)


def dot(a, b, dims):
    return lax.dot_general(a, b, dims, preferred_element_type=F32)


def row_of(z, xl, core):
    return (z * 2 + xl) * 2 + core


def col_of(y, xh):
    return y * 2 + xh


def kernel(
    x_ref, g_ref, q_ref, k_ref, v_ref, mask_ref, kb_ref, wq_ref, wk_ref, wv_ref,
    layer_out, dwq_out, dwk_out, dwv_out, bias_out,
    grads, xt, xt_send, dw, wt, mcol,
    part, got1, send2, got2, own2, last, landed, bias_send, bias_got,
    g_recv, g_send, xs_send, xs_recv, xt_recv, xt_ssem,
    r1_send, r1_recv, r2_send, r2_recv, f_send, f_recv, b_send, b_recv,
):
    row = lax.axis_index("row")
    col = lax.axis_index("col")
    z = lax.div(row, 4)
    xl = lax.rem(lax.div(row, 2), 2)
    core = lax.rem(row, 2)
    y = lax.div(col, 2)
    xh = lax.rem(col, 2)
    up, down = lax.rem(z + 1, 4), lax.rem(z + 3, 4)
    scale = 1.0 / (HD ** 0.5)
    sends = []

    def remote(src, dst, ssem, rsem, to):
        return pltpu.make_async_remote_copy(
            src_ref=src, dst_ref=dst, send_sem=ssem, recv_sem=rsem, device_id=to, device_id_type=MESH_ID
        )

    def chunk(r, ch):
        return grads.at[r, ch // 2, ch % 2]

    def g_copy(r, ch, to_row, slot):
        return remote(chunk(r, ch), chunk(r, ch), g_send.at[slot], g_recv.at[r, ch], (to_row, col))

    def g_put(r, ch, to_row):
        slot = len(sends)
        copy = g_copy(r, ch, to_row, slot)
        copy.start()
        sends.append((r, ch, to_row, slot))

    def g_wait(r, ch):
        g_copy(r, ch, row_of(z, xl, 1 - core), 0).wait_recv()

    to_up = row_of(up, xl, core)
    to_down = row_of(down, xl, core)
    to_x = row_of(z, 1 - xl, core)
    to_sib = row_of(z, xl, 1 - core)

    sources = {
        (dz, dx): row_of(lax.rem(z + dz, 4), lax.rem(xl + dx, 2), core) for dz in range(4) for dx in range(2)
    }

    def src(dz, dx):
        return sources[dz, dx]

    def from_z(dx, ch):
        low, high = src(3, dx), src(1, dx)
        for r, way in ((low, to_up if ch % 2 == 0 else None), (high, to_down if ch % 2 == 1 else None)):
            g_wait(r, ch)
            if way is not None:
                g_put(r, ch, way)
            if dx == 0 and ch in Z_FIRST:
                g_put(r, ch, to_x)
            g_put(r, ch, to_sib)

    def from_x(ch):
        r = src(0, 1)
        g_wait(r, ch)
        g_put(r, ch, to_up)
        g_put(r, ch, to_down)
        g_put(r, ch, to_sib)

    def far_x(dz, ch):
        r = src(dz, 1)
        g_wait(r, ch)
        g_put(r, ch, to_sib)

    def far_z(dx, ch):
        r = src(2, dx)
        g_wait(r, ch)
        if dx == 0 and ch in Z_FIRST:
            g_put(r, ch, to_x)
        g_put(r, ch, to_sib)

    x_sends = []

    def x_half(s, hs):
        return xt.at[s, pl.ds(hs * 2, 2)]

    def x_copy(s, hs, to_col, slot):
        return remote(x_half(s, hs), x_half(s, hs), xt_ssem.at[slot], xt_recv.at[s, hs], (row, to_col))

    def x_put(s, hs, to_col):
        slot = len(x_sends)
        x_copy(s, hs, to_col, slot).start()
        x_sends.append((s, hs, to_col, slot))

    def x_wait(s, hs):
        x_copy(s, hs, col_of(y, 1 - xh), 0).wait_recv()

    y_up, y_down = lax.rem(y + 1, 4), lax.rem(y + 3, 4)

    def x_first(h, k):
        to_row = row_of(y, xh, k)
        to_col = col_of(2 * core + h, xl)
        here = (to_row == row) & (to_col == col)

        def away():
            return remote(
                xt_send.at[h, k], xt.at[to_col, z], xs_send.at[h, k], xs_recv.at[z], (to_row, to_col)
            )

        def near():
            return pltpu.make_async_copy(xt_send.at[h, k], xt.at[to_col, z], xs_recv.at[z])

        return here, away, near

    def x_first_start(h, k):
        here, away, near = x_first(h, k)

        @pl.when(here)
        def _():
            near().start()

        @pl.when(jnp.logical_not(here))
        def _():
            away().start()

    def x_first_sent(h, k):
        here, away, _ = x_first(h, k)

        @pl.when(jnp.logical_not(here))
        def _():
            away().wait_send()

    def x_own():
        for zs in range(4):
            piece = xt.at[col, zs]
            pltpu.make_async_copy(piece, piece, xs_recv.at[zs]).wait()
        for hs in range(2):
            x_put(col, hs, col_of(y, 1 - xh))
            x_put(col, hs, col_of(y_up, xh))
            x_put(col, hs, col_of(y_down, xh))

    def x_across():
        other = col_of(y, 1 - xh)
        for hs in range(2):
            x_wait(other, hs)
            x_put(other, hs, col_of(y_up, xh))
            x_put(other, hs, col_of(y_down, xh))

    def x_near(xhs):
        for hs in range(2):
            low, high = col_of(y_down, xhs), col_of(y_up, xhs)
            x_wait(low, hs)
            if hs == 0:
                x_put(low, hs, col_of(y_up, xh))
            x_wait(high, hs)
            if hs == 1:
                x_put(high, hs, col_of(y_down, xh))

    def x_far(xhs):
        for hs in range(2):
            x_wait(col_of(lax.rem(y + 2, 4), xhs), hs)

    bias_to = (
        to_sib,
        to_x,
        row_of(z + 1 - 2 * lax.rem(z, 2), xl, core),
        row_of(lax.rem(z + 2, 4), xl, core),
    )

    def bias_copy(level):
        return remote(
            bias_send.at[level], bias_got.at[level], b_send.at[level], b_recv.at[level], (bias_to[level], col)
        )

    def bias_step(level):
        bias_copy(level).wait_recv()
        total = bias_send[level] + bias_got[level]
        if level < 3:
            bias_send[level + 1] = total
            bias_copy(level + 1).start()
        else:
            bias_out[...] = total[:1, :HEADS]

    for h in range(2):
        for k in range(2):
            xt_send[h, k] = x_ref[h * HALF:(h + 1) * HALF, k * DEPTH:(k + 1) * DEPTH].T
            x_first_start(h, k)
    mcol[...] = jnp.broadcast_to(mask_ref[...].astype(F32), (128, TOK)).T
    bias_send[0] = jnp.zeros((8, 128), F32)

    def head(h, carry):
        at = pl.ds(pl.multiple_of(h * HD, HD), HD)
        q, k, v, g = q_ref[:, at], k_ref[:, at], v_ref[:, at], g_ref[:, at]
        flag = jnp.concatenate([mcol[...], mcol[...]], axis=1)
        scores = dot(k, q, NT) * scale + flag * kb_ref[h]
        terms = jnp.exp(scores - jnp.max(scores, axis=0, keepdims=True))
        probs = terms * (1.0 / jnp.sum(terms, axis=0, keepdims=True))
        low = probs.astype(BF)
        grad_probs = dot(v, g, NT)
        delta = jnp.sum(low.astype(F32) * grad_probs, axis=0, keepdims=True)
        grad_scores = probs * (grad_probs - delta)
        grad_low = grad_scores.astype(BF)
        part_sum = jnp.sum(jnp.sum(grad_scores * flag, axis=0, keepdims=True), axis=1, keepdims=True)
        lane = lax.broadcasted_iota(jnp.int32, (8, 128), 1)
        bias_send[0] = bias_send[0] + jnp.where(lane == h, jnp.broadcast_to(part_sum, (8, 128)), 0.0)
        query_grad = (dot(grad_low, k, TN) * scale).astype(BF)
        key_grad = (dot(grad_low, q, NN) * scale).astype(BF)
        value_grad = dot(low, g, NN).astype(BF)
        for a, member in enumerate((query_grad, key_grad, value_grad)):
            for half in range(2):
                grads[row, a, half, :, at] = member[half * HALF:(half + 1) * HALF]
        return carry

    lax.fori_loop(0, HEADS, head, 0)

    for ch in X_FIRST:
        g_put(row, ch, to_x)
    for ch in ALL:
        g_put(row, ch, to_up)
        g_put(row, ch, to_down)
    for ch in Z_FIRST:
        g_put(row, ch, to_x)
    for ch in ALL:
        g_put(row, ch, to_sib)
    bias_copy(0).start()
    x_own()

    for a, w_ref in enumerate((wq_ref, wk_ref, wv_ref)):
        wt[a] = w_ref[...].T
    def clear(t, carry):
        dw[lax.div(t, 4), :, pl.ds(pl.multiple_of(lax.rem(t, 4) * 256, 256), 256)] = jnp.zeros((DEPTH, 256), F32)
        return carry

    lax.fori_loop(0, 12, clear, 0)

    from_x(2)
    from_z(0, 0)
    bias_step(0)
    x_across()
    from_x(3)
    from_z(0, 1)
    bias_step(1)
    x_near(xh)
    from_x(4)
    from_z(0, 2)
    from_x(5)
    from_z(0, 3)
    bias_step(2)
    x_near(1 - xh)
    from_z(0, 4)
    far_x(0, 0)
    from_z(0, 5)
    far_x(0, 1)
    bias_step(3)
    x_far(xh)
    x_far(1 - xh)

    def both_x(ch):
        far_x(1, ch)
        far_x(3, ch)

    events = {
        (0, 1): [lambda: far_z(0, 0)],
        (1, 0): [lambda: both_x(0)],
        (1, 1): [lambda: far_z(0, 1), lambda: from_z(1, 2)],
        (2, 0): [lambda: both_x(1)],
        (2, 1): [lambda: from_z(1, 3)],
        (3, 0): [lambda: far_z(0, 2), lambda: far_z(0, 3)],
        (3, 1): [lambda: from_z(1, 4)],
        (4, 0): [lambda: from_z(1, 5)],
        (4, 1): [lambda: far_x(2, 0)],
        (5, 0): [lambda: far_x(2, 1)],
        (6, 0): [lambda: far_z(0, 4), lambda: far_z(0, 5)],
        (7, 0): [lambda: far_z(1, 2), lambda: far_z(1, 3), lambda: far_z(1, 4), lambda: far_z(1, 5)],
    }

    def place(j):
        late = lax.div(j, 6)
        k = lax.rem(j, 3)
        dx = (1 - late) * lax.div(j, 3) + late * (j - 6)
        dz = (1 - late) * (k + lax.div(k, 2)) + late * 2
        return lax.rem(z + dz, 4), lax.rem(xl + dx, 2)

    def copy1(j, d):
        there = lax.rem(y + d, 4)
        return remote(
            part.at[j, there], got1.at[j, d - 1], r1_send.at[j, d - 1], r1_recv.at[j, d - 1],
            (row, col_of(there, xh)),
        )

    def copy2(j):
        return remote(send2.at[j], got2.at[j], r2_send.at[j], r2_recv.at[j], (row, col_of(y, 1 - xh)))

    def copy3(j, cs):
        zs, xs = place(j)
        to_row, to_col = row_of(zs, xs, cs), lax.div(row, 2)
        here = (to_row == row) & (to_col == col)
        k = lax.rem(row, 2)

        def away():
            return remote(
                last.at[j, cs], landed.at[k, col], f_send.at[j, cs], f_recv.at[k, col], (to_row, to_col)
            )

        def near():
            return pltpu.make_async_copy(last.at[j, cs], landed.at[k, col], f_recv.at[k, col])

        return here, away, near

    mine = pl.ds(pl.multiple_of(xh * 32, 32), 32)
    theirs = pl.ds(pl.multiple_of((1 - xh) * 32, 32), 32)

    def sum1(j):
        for d in (1, 2, 3):
            copy1(j, d).wait_recv()

        def over(at):
            total = part[j, y, :, at, :].astype(F32)
            for d in range(3):
                total = total + got1[j, d, :, at, :].astype(F32)
            return total

        send2[j] = over(theirs).astype(BF)
        copy2(j).start()
        own2[j] = over(mine)

    def sum2(j):
        copy2(j).wait_recv()
        last[j] = (own2[j] + got2[j].astype(F32)).astype(BF)
        for cs in range(2):
            here, away, near = copy3(j, cs)

            @pl.when(here)
            def _():
                near().start()

            @pl.when(jnp.logical_not(here))
            def _():
                away().start()

    def step(j, carry):
        for (at, half), todo in events.items():
            if half == 0:
                @pl.when(j == at)
                def _():
                    for one in todo:
                        one()
        zs, xs = place(j)
        for ch in ALL:
            g_wait(row_of(zs, xs, 1 - core), ch)
        for cs in range(2):
            r = row_of(zs, xs, cs)
            for n in range(2):
                total = None
                for a in range(3):
                    term = dot(
                        grads[r, a].reshape(TOK, WIDTH), wt[a, :, n * 256:(n + 1) * 256], NN
                    )
                    total = term if total is None else total + term
                part[j, :, cs, :, n * 256:(n + 1) * 256] = total.astype(BF).reshape(4, 64, 256)
        for d in (2, 1, 3):
            copy1(j, d).start()

        @pl.when(j >= 2)
        def _():
            sum2(j - 2)

        @pl.when(j >= 1)
        def _():
            sum1(j - 1)

        for (at, half), todo in events.items():
            if half == 1:
                @pl.when(j == at)
                def _():
                    for one in todo:
                        one()

        left = jnp.concatenate([xt[y4 * 2 + xs, zs] for y4 in range(4)], axis=1)

        for a in range(3):
            for n in range(4):
                cols = slice(n * 256, (n + 1) * 256)
                r0, r1 = row_of(zs, xs, 0), row_of(zs, xs, 1)
                right = jnp.concatenate(
                    [grads[r0, a, :, :, cols].reshape(TOK, 256), grads[r1, a, :, :, cols].reshape(TOK, 256)], axis=0
                )
                dw[a, :, cols] = dw[a, :, cols] + dot(left, right, NN)
        return carry

    lax.fori_loop(0, PAIRS, step, 0)

    sum2(PAIRS - 2)
    sum1(PAIRS - 1)
    for a, out in enumerate((dwq_out, dwk_out, dwv_out)):
        for n in range(4):
            out[:, n * 256:(n + 1) * 256] = dw[a, :, n * 256:(n + 1) * 256].astype(BF)
    sum2(PAIRS - 1)

    for r, ch, to_row, slot in sends:
        g_copy(r, ch, to_row, slot).wait_send()
    for s, hs, to_col, slot in x_sends:
        x_copy(s, hs, to_col, slot).wait_send()
    for h in range(2):
        for k in range(2):
            x_first_sent(h, k)
    for level in range(4):
        bias_copy(level).wait_send()

    def sent(j, carry):
        for d in (1, 2, 3):
            copy1(j, d).wait_send()
        copy2(j).wait_send()
        for cs in range(2):
            here, away, _ = copy3(j, cs)

            @pl.when(jnp.logical_not(here))
            def _():
                away().wait_send()
        return carry

    lax.fori_loop(0, PAIRS, sent, 0)
    for k in range(2):
        for s in range(COLS):
            piece = landed.at[k, s]
            pltpu.make_async_copy(piece, piece, f_recv.at[k, s]).wait()
            layer_out[s * 32:(s + 1) * 32, k * DEPTH:(k + 1) * DEPTH] = landed[k, s]


def local(layer_input, attn_grad, queries, keys, values, masked, key_bias, w_query, w_key, w_value):
    vmem = pl.BlockSpec(memory_space=pltpu.VMEM)
    smem = pl.BlockSpec(memory_space=pltpu.SMEM)
    dma = pltpu.SemaphoreType.DMA
    outs = pl.pallas_call(
        kernel,
        out_shape=(
            jax.ShapeDtypeStruct((TOK, WIDTH), BF),
            jax.ShapeDtypeStruct((DEPTH, WIDTH), BF),
            jax.ShapeDtypeStruct((DEPTH, WIDTH), BF),
            jax.ShapeDtypeStruct((DEPTH, WIDTH), BF),
            jax.ShapeDtypeStruct((1, HEADS), F32),
        ),
        in_specs=[vmem] * 6 + [smem] + [vmem] * 3,
        out_specs=(vmem,) * 5,
        scratch_shapes=[
            pltpu.VMEM((ROWS, 3, 2, HALF, WIDTH), BF),
            pltpu.VMEM((COLS, 4, DEPTH, HALF), BF),
            pltpu.VMEM((2, 2, DEPTH, HALF), BF),
            pltpu.VMEM((3, DEPTH, WIDTH), F32),
            pltpu.VMEM((3, WIDTH, DEPTH), BF),
            pltpu.VMEM((TOK, 128), F32),
            pltpu.VMEM((PAIRS, 4, 2, 64, DEPTH), BF),
            pltpu.VMEM((PAIRS, 3, 2, 64, DEPTH), BF),
            pltpu.VMEM((PAIRS, 2, 32, DEPTH), BF),
            pltpu.VMEM((PAIRS, 2, 32, DEPTH), BF),
            pltpu.VMEM((PAIRS, 2, 32, DEPTH), F32),
            pltpu.VMEM((PAIRS, 2, 32, DEPTH), BF),
            pltpu.VMEM((2, COLS, 32, DEPTH), BF),
            pltpu.VMEM((4, 8, 128), F32),
            pltpu.VMEM((4, 8, 128), F32),
            dma((ROWS, 6)),
            dma((96,)),
            dma((2, 2)),
            dma((4,)),
            dma((COLS, 2)),
            dma((16,)),
            dma((PAIRS, 3)),
            dma((PAIRS, 3)),
            dma((PAIRS,)),
            dma((PAIRS,)),
            dma((PAIRS, 2)),
            dma((2, COLS)),
            dma((4,)),
            dma((4,)),
        ],
        compiler_params=pltpu.CompilerParams(has_side_effects=True, vmem_limit_bytes=62 * 2**20),
    )(
        layer_input, attn_grad, queries[0], keys[0], values[0], masked, key_bias, w_query, w_key, w_value
    )
    return outs[0], outs[1], outs[2], outs[3], outs[4].reshape(HEADS)


def solution(mesh):
    in_specs = (
        P("row", "col"),
        P("row", "col"),
        P("row", None, "col"),
        P("row", None, "col"),
        P("row", None, "col"),
        P("row", None),
        P("col"),
        P("row", "col"),
        P("row", "col"),
        P("row", "col"),
    )
    out_specs = (P("row", "col"), P("row", "col"), P("row", "col"), P("row", "col"), P("col"))
    return jax.shard_map(local, mesh=mesh, in_specs=in_specs, out_specs=out_specs, check_vma=False)
```

```python
import functools

import jax
import jax.numpy as jnp
from jax import lax
from jax.experimental import pallas as pl
from jax.experimental.pallas import tpu as pltpu
from jax.sharding import PartitionSpec as P

BF = jnp.bfloat16
F32 = jnp.float32
MESH_ID = pl.DeviceIdType.MESH

ROWS, COLS = 16, 8
TOK, WIDTH, DEPTH = 256, 1024, 512
HEADS, HD = 8, 128
HALF = TOK // 2
SPLIT = WIDTH // 2
PAIRS = 8
NT = (((1,), (1,)), ((), ()))
TN = (((0,), (0,)), ((), ()))
NN = (((1,), (0,)), ((), ()))

Z_FIRST = (0, 1)
ALL = (0, 2, 4, 1, 3, 5)
X_FIRST = tuple(ch for ch in ALL if ch not in Z_FIRST)

BEFORE = (
    ("attend", 0), ("start",), ("own", "d", 4), ("own", "d", 2), ("attend", 1), ("own", "u", 4),
    ("own", "u", 5), ("own", "x", 3), ("own", "d", 0), ("own", "u", 0), ("own", "d", 1), ("own", "u", 2),
    ("own", "x", 5), ("own", "u", 1), ("x_arrived",), ("x_over",), ("x_round",), ("own", "s", 4),
    ("own", "d", 3), ("own", "u", 3), ("own", "s", 3), ("from_z", 0, 4), ("own", "x", 2), ("x_near", 0),
    ("own", "x", 4), ("x_across", 0), ("own", "x", 0), ("from_z", 0, 2), ("own", "d", 5), ("prepare",),
    ("own", "x", 1), ("x_across", 1), ("from_x", 2), ("from_x", 5), ("own", "s", 2), ("from_z", 0, 0),
    ("from_z", 0, 1), ("from_z", 0, 3), ("x_near", 1), ("hop", 0, 0), ("from_z", 0, 5), ("own", "s", 5),
    ("hop", 0, 3), ("x_far", 0), ("own", "s", 1), ("from_x", 3),
)
STEPS = (
    ("D", 2, (
    )),
    ("D", 1, (
        ("from_x", 4), ("own", "s", 0), ("hop", 0, 4),
    )),
    ("W", 2, (
        ("x_far", 1), ("far_x", 0, 0), ("far_x", 0, 1), ("hop", 0, 5), ("bias", 0),
    )),
    ("D", 3, (
    )),
    ("D", 0, (
        ("hop", 0, 2), ("hop", 0, 1), ("far_x", 3, 0),
    )),
    ("W", 3, (
        ("from_z", 1, 5),
    )),
    ("W", 0, (
        ("from_z", 1, 2), ("bias", 1),
    )),
    ("W", 1, (
    )),
    ("D", 5, (
        ("sum1", 2), ("far_z", 0, 3), ("from_z", 1, 4), ("far_z", 0, 0), ("far_x", 3, 1), ("from_z", 1, 3),
        ("sum1", 3), ("far_x", 1, 0), ("far_z", 0, 5), ("far_x", 1, 1),
    )),
    ("W", 5, (
    )),
    ("D", 4, (
        ("bias", 2),
    )),
    ("W", 4, (
        ("sum2", 2), ("far_x", 2, 0), ("far_z", 0, 4), ("far_z", 0, 2), ("far_z", 0, 1),
    )),
    ("D", 6, (
        ("far_z", 1, 5), ("far_z", 1, 2), ("sum1", 0),
    )),
    ("D", 7, (
        ("sum2", 3), ("far_x", 2, 1), ("sum1", 1), ("sum1", 5), ("sum2", 0), ("far_z", 1, 4), ("far_z", 1, 3),
        ("sum1", 4), ("sum2", 1),
    )),
    ("W", 7, (
        ("sum1", 6), ("bias", 3),
    )),
    ("W", 6, (
    )),
)
AFTER = (
    ("sum2", 5), ("sum2", 4), ("sum2", 6), ("sum1", 7), ("sum2", 7),
)


def dot(a, b, dims):
    return lax.dot_general(a, b, dims, preferred_element_type=F32)


def row_of(z, xl, core):
    return (z * 2 + xl) * 2 + core


def col_of(y, xh):
    return y * 2 + xh


def kernel(
    x_ref, g_ref, q_ref, k_ref, v_ref, mask_ref, kb_ref, wq_ref, wk_ref, wv_ref,
    layer_out, dwq_out, dwk_out, dwv_out, bias_out,
    grads, xt, xt_send, dw, wt, mcol,
    part, got1, send2, got2, own2, last, landed, bias_send, bias_got,
    g_recv, g_send, xs_send, xs_recv, xt_recv, xt_ssem,
    r1_send, r1_recv, r2_send, r2_recv, f_send, f_recv, b_send, b_recv,
):
    row = lax.axis_index("row")
    col = lax.axis_index("col")
    z = lax.div(row, 4)
    xl = lax.rem(lax.div(row, 2), 2)
    core = lax.rem(row, 2)
    y = lax.div(col, 2)
    xh = lax.rem(col, 2)
    up, down = lax.rem(z + 1, 4), lax.rem(z + 3, 4)
    scale = 1.0 / (HD ** 0.5)
    sends = []

    def remote(src, dst, ssem, rsem, to):
        return pltpu.make_async_remote_copy(
            src_ref=src, dst_ref=dst, send_sem=ssem, recv_sem=rsem, device_id=to, device_id_type=MESH_ID
        )

    def chunk(r, ch):
        return grads.at[r, ch // 2, ch % 2]

    def g_copy(r, ch, to_row, slot):
        return remote(chunk(r, ch), chunk(r, ch), g_send.at[slot], g_recv.at[r, ch], (to_row, col))

    def g_put(r, ch, to_row):
        slot = len(sends)
        copy = g_copy(r, ch, to_row, slot)
        copy.start()
        sends.append((r, ch, to_row, slot))

    def g_wait(r, ch):
        g_copy(r, ch, row_of(z, xl, 1 - core), 0).wait_recv()

    to_up = row_of(up, xl, core)
    to_down = row_of(down, xl, core)
    to_x = row_of(z, 1 - xl, core)
    to_sib = row_of(z, xl, 1 - core)

    sources = {
        (dz, dx): row_of(lax.rem(z + dz, 4), lax.rem(xl + dx, 2), core) for dz in range(4) for dx in range(2)
    }

    def src(dz, dx):
        return sources[dz, dx]

    def hop(dx, ch):
        if ch % 2 == 0:
            g_put(src(3, dx), ch, to_up)
        else:
            g_put(src(1, dx), ch, to_down)

    def from_z(dx, ch):
        if dx == 1:
            g_wait(src(1 if ch % 2 else 3, 1), ch)
            hop(1, ch)
            g_wait(src(3 if ch % 2 else 1, 1), ch)
        for r in (src(3, dx), src(1, dx)):
            if dx == 0:
                g_wait(r, ch)
            if dx == 0 and ch in Z_FIRST:
                g_put(r, ch, to_x)
            g_put(r, ch, to_sib)

    def from_x(ch):
        r = src(0, 1)
        g_wait(r, ch)
        g_put(r, ch, to_up)
        g_put(r, ch, to_down)
        g_put(r, ch, to_sib)

    def far_x(dz, ch):
        r = src(dz, 1)
        g_wait(r, ch)
        g_put(r, ch, to_sib)

    def far_z(dx, ch):
        r = src(2, dx)
        g_wait(r, ch)
        if dx == 0 and ch in Z_FIRST:
            g_put(r, ch, to_x)
        g_put(r, ch, to_sib)

    x_sends = []

    def x_half(s, hs):
        return xt.at[s, pl.ds(hs * 2, 2)]

    def x_copy(s, hs, to_col, slot):
        return remote(x_half(s, hs), x_half(s, hs), xt_ssem.at[slot], xt_recv.at[s, hs], (row, to_col))

    def x_put(s, hs, to_col):
        slot = len(x_sends)
        x_copy(s, hs, to_col, slot).start()
        x_sends.append((s, hs, to_col, slot))

    def x_wait(s, hs):
        x_copy(s, hs, col_of(y, 1 - xh), 0).wait_recv()

    y_up, y_down = lax.rem(y + 1, 4), lax.rem(y + 3, 4)

    def x_first(h, k):
        to_row = row_of(y, xh, k)
        to_col = col_of(2 * core + h, xl)
        here = (to_row == row) & (to_col == col)

        def away():
            return remote(
                xt_send.at[h, k], xt.at[to_col, z], xs_send.at[h, k], xs_recv.at[z], (to_row, to_col)
            )

        def near():
            return pltpu.make_async_copy(xt_send.at[h, k], xt.at[to_col, z], xs_recv.at[z])

        return here, away, near

    def x_first_start(h, k):
        here, away, near = x_first(h, k)

        @pl.when(here)
        def _():
            near().start()

        @pl.when(jnp.logical_not(here))
        def _():
            away().start()

    def x_first_sent(h, k):
        here, away, _ = x_first(h, k)

        @pl.when(jnp.logical_not(here))
        def _():
            away().wait_send()

    def x_arrived():
        for zs in range(4):
            piece = xt.at[col, zs]
            pltpu.make_async_copy(piece, piece, xs_recv.at[zs]).wait()

    def x_over():
        for hs in range(2):
            x_put(col, hs, col_of(y, 1 - xh))

    def x_round():
        for hs in range(2):
            x_put(col, hs, col_of(y_up, xh))
            x_put(col, hs, col_of(y_down, xh))

    def x_across(hs):
        other = col_of(y, 1 - xh)
        x_wait(other, hs)
        x_put(other, hs, col_of(y_up, xh))
        x_put(other, hs, col_of(y_down, xh))

    def x_near(other):
        xhs = 1 - xh if other else xh
        for hs in range(2):
            low, high = col_of(y_down, xhs), col_of(y_up, xhs)
            x_wait(low, hs)
            if hs == 0:
                x_put(low, hs, col_of(y_up, xh))
            x_wait(high, hs)
            if hs == 1:
                x_put(high, hs, col_of(y_down, xh))

    def x_far(other):
        xhs = 1 - xh if other else xh
        for hs in range(2):
            x_wait(col_of(lax.rem(y + 2, 4), xhs), hs)

    bias_to = (
        to_sib,
        to_x,
        row_of(z + 1 - 2 * lax.rem(z, 2), xl, core),
        row_of(lax.rem(z + 2, 4), xl, core),
    )

    def bias_copy(level):
        return remote(
            bias_send.at[level], bias_got.at[level], b_send.at[level], b_recv.at[level], (bias_to[level], col)
        )

    def bias_step(level):
        bias_copy(level).wait_recv()
        total = bias_send[level] + bias_got[level]
        if level < 3:
            bias_send[level + 1] = total
            bias_copy(level + 1).start()
        else:
            bias_out[...] = total[:1, :HEADS]

    ready = pltpu.get_barrier_semaphore()
    for to in (
        (to_up, col), (to_down, col), (row_of(lax.rem(z + 2, 4), xl, core), col), (to_x, col), (to_sib, col),
        (row, col_of(y_up, xh)), (row, col_of(y_down, xh)), (row, col_of(lax.rem(y + 2, 4), xh)),
        (row, col_of(y, 1 - xh)),
    ):
        pl.semaphore_signal(ready, inc=1, device_id=to, device_id_type=MESH_ID)
    for zs in range(4):
        from_row, from_col = row_of(zs, xh, lax.div(y, 2)), col_of(z, xl)
        itself = (from_row == row) & (from_col == col)

        @pl.when(jnp.logical_not(itself))
        def _():
            pl.semaphore_signal(ready, inc=1, device_id=(from_row, from_col), device_id_type=MESH_ID)

    for h in range(2):
        for k in range(2):
            xt_send[h, k] = x_ref[h * HALF:(h + 1) * HALF, k * DEPTH:(k + 1) * DEPTH].T
    mcol[...] = jnp.broadcast_to(mask_ref[...].astype(F32), (128, TOK)).T
    bias_send[0] = jnp.zeros((8, 128), F32)

    def head(half, n, carry):
        h = half * 4 + n
        at = pl.ds(pl.multiple_of(h * HD, HD), HD)
        to = pl.ds(pl.multiple_of(n * HD, HD), HD)
        q, k, v, g = q_ref[:, at], k_ref[:, at], v_ref[:, at], g_ref[:, at]
        flag = jnp.concatenate([mcol[...], mcol[...]], axis=1)
        scores = dot(k, q, NT) * scale + flag * kb_ref[h]
        terms = jnp.exp(scores - jnp.max(scores, axis=0, keepdims=True))
        probs = terms * (1.0 / jnp.sum(terms, axis=0, keepdims=True))
        low = probs.astype(BF)
        grad_probs = dot(v, g, NT)
        delta = jnp.sum(low.astype(F32) * grad_probs, axis=0, keepdims=True)
        grad_scores = probs * (grad_probs - delta)
        grad_low = grad_scores.astype(BF)
        part_sum = jnp.sum(jnp.sum(grad_scores * flag, axis=0, keepdims=True), axis=1, keepdims=True)
        lane = lax.broadcasted_iota(jnp.int32, (8, 128), 1)
        bias_send[0] = bias_send[0] + jnp.where(lane == h, jnp.broadcast_to(part_sum, (8, 128)), 0.0)
        query_grad = (dot(grad_low, k, TN) * scale).astype(BF)
        key_grad = (dot(grad_low, q, NN) * scale).astype(BF)
        value_grad = dot(low, g, NN).astype(BF)
        for a, member in enumerate((query_grad, key_grad, value_grad)):
            grads[row, a, half, :, to] = member
        return carry

    def place(j):
        late = lax.div(j, 6)
        k = lax.rem(j, 3)
        dx = (1 - late) * lax.div(j, 3) + late * (j - 6)
        dz = (1 - late) * (k + lax.div(k, 2)) + late * 2
        return lax.rem(z + dz, 4), lax.rem(xl + dx, 2)

    def copy1(j, d):
        there = lax.rem(y + d, 4)
        return remote(
            part.at[j, there], got1.at[j, d - 1], r1_send.at[j, d - 1], r1_recv.at[j, d - 1],
            (row, col_of(there, xh)),
        )

    def copy2(j):
        return remote(send2.at[j], got2.at[j], r2_send.at[j], r2_recv.at[j], (row, col_of(y, 1 - xh)))

    def copy3(j, cs):
        zs, xs = place(j)
        to_row, to_col = row_of(zs, xs, cs), lax.div(row, 2)
        here = (to_row == row) & (to_col == col)
        k = lax.rem(row, 2)

        def away():
            return remote(
                last.at[j, cs], landed.at[k, col], f_send.at[j, cs], f_recv.at[k, col], (to_row, to_col)
            )

        def near():
            return pltpu.make_async_copy(last.at[j, cs], landed.at[k, col], f_recv.at[k, col])

        return here, away, near

    mine = pl.ds(pl.multiple_of(xh * 32, 32), 32)
    theirs = pl.ds(pl.multiple_of((1 - xh) * 32, 32), 32)

    def sum1(j):
        for d in (1, 2, 3):
            copy1(j, d).wait_recv()

        def over(at):
            total = part[j, y, :, at, :].astype(F32)
            for d in range(3):
                total = total + got1[j, d, :, at, :].astype(F32)
            return total

        send2[j] = over(theirs).astype(BF)
        copy2(j).start()
        own2[j] = over(mine)

    def sum2(j):
        copy2(j).wait_recv()
        last[j] = (own2[j] + got2[j].astype(F32)).astype(BF)
        for cs in range(2):
            here, away, near = copy3(j, cs)

            @pl.when(here)
            def _():
                near().start()

            @pl.when(jnp.logical_not(here))
            def _():
                away().start()

    def input_part(j):
        zs, xs = place(j)
        for ch in ALL:
            g_wait(row_of(zs, xs, 1 - core), ch)
        for cs in range(2):
            r = row_of(zs, xs, cs)
            left = jnp.concatenate([grads[r, a, half] for a in range(3) for half in range(2)], axis=1)
            for n in range(2):
                cols = slice(n * 256, (n + 1) * 256)
                part[j, :, cs, :, cols] = dot(left, wt[:, cols], NN).astype(BF).reshape(4, 64, 256)
        for d in (1, 3, 2):
            copy1(j, d).start()

    def weight_part(j):
        zs, xs = place(j)
        left = jnp.concatenate([xt[y4 * 2 + xs, zs] for y4 in range(4)], axis=1)
        r0, r1 = row_of(zs, xs, 0), row_of(zs, xs, 1)
        for a in range(3):
            for n in range(4):
                cols = slice(n * 256, (n + 1) * 256)
                within = slice((n % 2) * 256, (n % 2 + 1) * 256)
                right = jnp.concatenate([grads[r, a, n // 2, :, within] for r in (r0, r1)], axis=0)
                dw[a, :, cols] = dw[a, :, cols] + dot(left, right, NN)

    def start_sends():
        one_is_here = (y == z) & (xh == xl) & (lax.div(y, 2) == core)
        pl.semaphore_wait(ready, jnp.where(one_is_here, 12, 13))
        for h in range(2):
            for k in range(2):
                x_first_start(h, k)

    def attend(half):
        lax.fori_loop(0, HEADS // 2, functools.partial(head, half), 0)
        if half == 1:
            bias_copy(0).start()

    def prepare():
        for a, w_ref in enumerate((wq_ref, wk_ref, wv_ref)):
            wt[a * WIDTH:(a + 1) * WIDTH] = w_ref[...].T

        def clear(t, carry):
            cols = pl.ds(pl.multiple_of(lax.rem(t, 4) * 256, 256), 256)
            dw[lax.div(t, 4), :, cols] = jnp.zeros((DEPTH, 256), F32)
            return carry

        lax.fori_loop(0, 12, clear, 0)

    ways = {"u": to_up, "d": to_down, "x": to_x, "s": to_sib}
    does = {
        "attend": attend, "start": start_sends, "own": lambda way, ch: g_put(row, ch, ways[way]),
        "x_arrived": x_arrived, "x_over": x_over, "x_round": x_round, "x_across": x_across, "x_near": x_near,
        "x_far": x_far, "hop": hop, "from_z": from_z, "from_x": from_x, "far_x": far_x, "far_z": far_z,
        "sum1": sum1, "sum2": sum2, "prepare": prepare, "bias": bias_step,
    }

    def play(todo):
        for name, *rest in todo:
            does[name](*rest)

    play(BEFORE)

    def step(k, carry):
        for at, (_, _, todo) in enumerate(STEPS):
            if todo:
                @pl.when(k == at)
                def _():
                    play(todo)

        j = sum(jnp.where(k == at, what, 0) for at, (_, what, _) in enumerate(STEPS) if what)
        weights = sum(jnp.where(k == at, 1, 0) for at, (kind, _, _) in enumerate(STEPS) if kind == "W")

        @pl.when(weights == 0)
        def _():
            input_part(j)

        @pl.when(weights == 1)
        def _():
            weight_part(j)

        return carry

    lax.fori_loop(0, len(STEPS), step, 0)
    play(AFTER)
    for a, out in enumerate((dwq_out, dwk_out, dwv_out)):
        for n in range(4):
            out[:, n * 256:(n + 1) * 256] = dw[a, :, n * 256:(n + 1) * 256].astype(BF)

    for r, ch, to_row, slot in sends:
        g_copy(r, ch, to_row, slot).wait_send()
    for s, hs, to_col, slot in x_sends:
        x_copy(s, hs, to_col, slot).wait_send()
    for h in range(2):
        for k in range(2):
            x_first_sent(h, k)
    for level in range(4):
        bias_copy(level).wait_send()

    def sent(j, carry):
        for d in (1, 2, 3):
            copy1(j, d).wait_send()
        copy2(j).wait_send()
        for cs in range(2):
            here, away, _ = copy3(j, cs)

            @pl.when(jnp.logical_not(here))
            def _():
                away().wait_send()
        return carry

    lax.fori_loop(0, PAIRS, sent, 0)
    for k in range(2):
        for s in range(COLS):
            piece = landed.at[k, s]
            pltpu.make_async_copy(piece, piece, f_recv.at[k, s]).wait()
            layer_out[s * 32:(s + 1) * 32, k * DEPTH:(k + 1) * DEPTH] = landed[k, s]


def local(layer_input, attn_grad, queries, keys, values, masked, key_bias, w_query, w_key, w_value):
    vmem = pl.BlockSpec(memory_space=pltpu.VMEM)
    smem = pl.BlockSpec(memory_space=pltpu.SMEM)
    dma = pltpu.SemaphoreType.DMA
    outs = pl.pallas_call(
        kernel,
        out_shape=(
            jax.ShapeDtypeStruct((TOK, WIDTH), BF),
            jax.ShapeDtypeStruct((DEPTH, WIDTH), BF),
            jax.ShapeDtypeStruct((DEPTH, WIDTH), BF),
            jax.ShapeDtypeStruct((DEPTH, WIDTH), BF),
            jax.ShapeDtypeStruct((1, HEADS), F32),
        ),
        in_specs=[vmem] * 6 + [smem] + [vmem] * 3,
        out_specs=(vmem,) * 5,
        scratch_shapes=[
            pltpu.VMEM((ROWS, 3, 2, TOK, SPLIT), BF),
            pltpu.VMEM((COLS, 4, DEPTH, HALF), BF),
            pltpu.VMEM((2, 2, DEPTH, HALF), BF),
            pltpu.VMEM((3, DEPTH, WIDTH), F32),
            pltpu.VMEM((3 * WIDTH, DEPTH), BF),
            pltpu.VMEM((TOK, 128), F32),
            pltpu.VMEM((PAIRS, 4, 2, 64, DEPTH), BF),
            pltpu.VMEM((PAIRS, 3, 2, 64, DEPTH), BF),
            pltpu.VMEM((PAIRS, 2, 32, DEPTH), BF),
            pltpu.VMEM((PAIRS, 2, 32, DEPTH), BF),
            pltpu.VMEM((PAIRS, 2, 32, DEPTH), F32),
            pltpu.VMEM((PAIRS, 2, 32, DEPTH), BF),
            pltpu.VMEM((2, COLS, 32, DEPTH), BF),
            pltpu.VMEM((4, 8, 128), F32),
            pltpu.VMEM((4, 8, 128), F32),
            dma((ROWS, 6)),
            dma((96,)),
            dma((2, 2)),
            dma((4,)),
            dma((COLS, 2)),
            dma((16,)),
            dma((PAIRS, 3)),
            dma((PAIRS, 3)),
            dma((PAIRS,)),
            dma((PAIRS,)),
            dma((PAIRS, 2)),
            dma((2, COLS)),
            dma((4,)),
            dma((4,)),
        ],
        compiler_params=pltpu.CompilerParams(collective_id=0, has_side_effects=True, vmem_limit_bytes=62 * 2**20),
    )(
        layer_input, attn_grad, queries[0], keys[0], values[0], masked, key_bias, w_query, w_key, w_value
    )
    return outs[0], outs[1], outs[2], outs[3], outs[4].reshape(HEADS)


def solution(mesh):
    in_specs = (
        P("row", "col"),
        P("row", "col"),
        P("row", None, "col"),
        P("row", None, "col"),
        P("row", None, "col"),
        P("row", None),
        P("col"),
        P("row", "col"),
        P("row", "col"),
        P("row", "col"),
    )
    out_specs = (P("row", "col"), P("row", "col"), P("row", "col"), P("row", "col"), P("col"))
    return jax.shard_map(local, mesh=mesh, in_specs=in_specs, out_specs=out_specs, check_vma=False)
```
